32 devices in a mesh: bra: 8 (over z, x), ket: 4 (over y, core).
Axes of the slice: x: 2, y: 2, z: 4, core: 2. Of those that a mesh axis runs over, the one named last changes fastest.
Arguments:
- densities: bfloat16 [8, 8, 40, 640], P('bra', 'ket'), may hold values from -6 to 6
- fit_factors: bfloat16 [8, 40, 256], replicated, may hold values from -1 to 1
- coupling: float32 [256, 256], replicated, may hold values from -0.5 to 2
- quartets: int32 [8, 4, 16, 3], P('bra', 'ket'), may hold values from 0 to 7, as said below
- live_count: int32 [8, 4], P('bra', 'ket'), may hold values from 0 to 16, as said below
Outputs:
- coulomb: bfloat16 [8, 8, 40, 640], P('bra', 'ket')
- exchange: bfloat16 [8, 8, 40, 640], P('bra', 'ket')
The draws below stay inside these ranges and needn't reach their ends.
Inputs may be any that keep to these rules, and one draw needn't show every extreme that they name: `quartets`: entry [i, j, t] gives blocks B, C, D of slot t of the device with bra index i and ket index j; its block A is i. Over the 16 slots of one device the B and C entries together name every block exactly 4 times, and D // 2 equals j. `live_count`: the counts of two devices with the same ket index whose bra indices differ by half of the bra axis sum to 16.
All inputs are finite; a program needn't handle non-finite values.
Results may differ from the reference program's by a relative error of at most 0.007.
Values may be sent and summed in bfloat16 or wider, within the bound.
A program may use at most 64 MiB of HBM per device.

```python
import jax
import jax.numpy as jnp
from jax import lax

B = 40
R = 256
KD = 16
CAP = 16
NBLK = 8
PC = 2
QSLOT = 4
N_BRA = 8
N_KET = 4


def draw_quartets(key, part):
    devices_all = N_BRA * N_KET
    keys = jax.random.split(key, devices_all)
    ket_ranks = jnp.arange(devices_all, dtype=jnp.int32) % N_KET
    pool = jnp.tile(jnp.arange(NBLK, dtype=jnp.int32), QSLOT)

    def one_list(dev_key, ket_rank):
        mixed = jax.random.permutation(jax.random.fold_in(dev_key, 11), pool)
        column = ket_rank * PC + jax.random.randint(jax.random.fold_in(dev_key, 12), (CAP,), 0, PC)
        return jnp.stack([mixed[:CAP], mixed[CAP:], column.astype(jnp.int32)], axis=1)
    lists = jax.vmap(one_list)(keys, ket_ranks)
    return lists.reshape(N_BRA, N_KET, CAP, 3).astype(jnp.int32)


def draw_live_count(key, part):
    half_bra = N_BRA // 2
    key_share = jax.random.fold_in(key, 21)
    key_pick = jax.random.fold_in(key, 22)
    key_flip = jax.random.fold_in(key, 23)
    share = jax.random.randint(key_share, (half_bra, N_KET), 0, CAP + 1)
    chosen = jax.random.randint(key_pick, (), 0, half_bra * N_KET)
    marker = jnp.arange(half_bra * N_KET, dtype=jnp.int32).reshape(half_bra, N_KET)
    share = jnp.where(marker == chosen, CAP, share)
    flipped = jax.random.randint(key_flip, (half_bra, N_KET), 0, 2)
    first = jnp.where(flipped == 1, share, CAP - share)
    return jnp.concatenate([first, CAP - first], axis=0).astype(jnp.int32)


def draw_coupling(key, part):
    key_diag = jax.random.fold_in(key, 31)
    key_off = jax.random.fold_in(key, 32)
    identity = jnp.eye(R, dtype=jnp.float32)
    diagonal = jax.random.uniform(key_diag, (R,), jnp.float32, 0.5, 1.5)
    offdiag = jnp.clip(0.08 * jax.random.normal(key_off, (R, R), jnp.float32), -0.3, 0.3)
    return (identity * diagonal[:, None] + (1.0 - identity) * offdiag).astype(jnp.float32)


def level_of(stream_key, dims, pieces, smallest, top_value):
    loudness, own = 1.0, jax.random.fold_in(stream_key, 6)
    for axis_at, shards_of in pieces:
        draws = jnp.exp(jax.random.uniform(jax.random.fold_in(own, axis_at), (shards_of,), jnp.float32, smallest / len(pieces), top_value / len(pieces)))
        loudness = loudness * jnp.repeat(draws, dims[axis_at] // shards_of).reshape([-1 if axis == axis_at else 1 for axis in range(len(dims))])
    return loudness


def centred(stream_key, dims, scale, limit, shards=(), kind=jnp.bfloat16):
    array = jax.random.normal(stream_key, dims, jnp.float32) * scale
    if len(shards) > 0:
        array = level_of(stream_key, dims, shards, -0.22, 0.18) * array
    return jnp.clip(array, min=-limit, max=limit).astype(kind)


def setup_inputs(seed: int = 0) -> dict:
    streams_of = jax.random.split(jax.random.key(seed), 6)
    densities = centred(streams_of[0], (NBLK, NBLK, B, B * KD), 1.0, 6.0, ((0, 8), (1, 4)))
    fit_factors = centred(streams_of[1], (NBLK, B, R), B ** -0.5, 1.0)
    coupling = draw_coupling(jax.random.fold_in(streams_of[5], 71), 0)
    quartets = draw_quartets(jax.random.fold_in(streams_of[5], 71), 0)
    live_count = draw_live_count(jax.random.fold_in(streams_of[5], 71), 0)
    return dict(densities=densities, fit_factors=fit_factors, coupling=coupling, quartets=quartets, live_count=live_count)


def quartet_terms(bra_left, bra_right, ket_left, ket_right, block_cd, block_bd, weight, coupling):
    single = jnp.float32
    width = bra_left.shape[0]
    dens_count = block_cd.shape[1] // width
    cube_cd = block_cd.astype(single).reshape(width, width, dens_count)
    ket_image = jnp.einsum('cdk,dq->ckq', cube_cd, ket_right.astype(single))
    fitted = jnp.sum(ket_left.astype(single)[:, None, :] * ket_image, axis=0)
    pushed = jnp.dot(fitted, coupling.T, precision=lax.Precision.HIGHEST)
    spread = (bra_left.astype(single)[:, None, :] * pushed[None, :, :]).astype(jnp.bfloat16)
    spread = lax.optimization_barrier(spread)
    coulomb_term = jnp.einsum('akp,bp->abk', spread.astype(single), bra_right.astype(single))
    coulomb_term = (weight * coulomb_term).reshape(width, width * dens_count).astype(jnp.bfloat16)
    cube_bd = block_bd.astype(single).reshape(width, width, dens_count)
    side_image = jnp.einsum('bdk,dq->bkq', cube_bd, ket_right.astype(single)).astype(jnp.bfloat16)
    side_image = lax.optimization_barrier(side_image)
    heavy = jnp.einsum('bp,bkq->pkq', bra_right.astype(single), side_image.astype(single))
    wide = (coupling[:, None, :] * heavy).astype(jnp.bfloat16)
    wide = lax.optimization_barrier(wide)
    narrow = jnp.einsum('ap,pkq->akq', bra_left.astype(single), wide.astype(single)).astype(jnp.bfloat16)
    narrow = lax.optimization_barrier(narrow)
    exchange_term = jnp.einsum('akq,cq->ack', narrow.astype(single), ket_left.astype(single))
    exchange_term = (weight * exchange_term).reshape(width, width * dens_count).astype(jnp.bfloat16)
    return coulomb_term, exchange_term


def reference(densities, fit_factors, coupling, quartets, live_count):
    devices_all = N_BRA * N_KET
    task_lists = quartets.reshape(devices_all, CAP, 3).astype(jnp.int32)
    row_owner = (jnp.arange(devices_all, dtype=jnp.int32) // N_KET).astype(jnp.int32)
    slot_ids = jnp.arange(CAP, dtype=jnp.int32)
    weights = (slot_ids[None, :] < live_count.reshape(devices_all)[:, None]).astype(jnp.float32)
    zero_acc = jnp.zeros((NBLK, NBLK, B, B * KD), jnp.float32)
    mapped = jax.vmap(quartet_terms, in_axes=(None, 0, 0, 0, 0, 0, 0, None))

    def step(carry, inputs):
        coul_acc, exch_acc = carry
        row_a, task, weight = inputs
        second = task[:, 0]
        ket_first = task[:, 1]
        ket_second = task[:, 2]
        coul, exch = mapped(fit_factors[row_a], fit_factors[second], fit_factors[ket_first],
                            fit_factors[ket_second], densities[ket_first, ket_second],
                            densities[second, ket_second], weight, coupling)
        rows_a = jnp.full((CAP,), row_a, jnp.int32)
        coul_acc = coul_acc.at[rows_a, second].add(coul.astype(jnp.float32))
        exch_acc = exch_acc.at[rows_a, ket_first].add(exch.astype(jnp.float32))
        return (coul_acc, exch_acc), None

    (coul_acc, exch_acc), unused = lax.scan(step, (zero_acc, zero_acc), (row_owner, task_lists, weights))
    return coul_acc.astype(jnp.bfloat16), exch_acc.astype(jnp.bfloat16)
```

```python
import functools

import jax
import jax.numpy as jnp
from jax import lax
from jax.experimental import pallas as pl
from jax.experimental.pallas import tpu as pltpu
from jax.sharding import PartitionSpec as P

MESH = pl.DeviceIdType.MESH


def kernel(dims, tasks_ref, live_ref, dens_ref, fit_ref, coup_ref, coul_ref, exch_ref,
           held, counts, factor, trans, image, inner, spread, term_out, term_in, fit_out, fit_in,
           hold_send, hold_recv, term_send, term_recv, fit_send, fit_recv):
    n_bra, n_ket, cols, width, dens_count, points, blocks, slots = dims
    flat = width * dens_count
    lanes = 128
    single, half = jnp.float32, jnp.bfloat16
    bra, ket = lax.axis_index("bra"), lax.axis_index("ket")

    barrier = pltpu.get_barrier_semaphore()
    for step in range(1, n_bra):
        pl.semaphore_signal(barrier, inc=1, device_id=(lax.rem(bra + step, n_bra), ket), device_id_type=MESH)
    for step in range(1, n_ket):
        pl.semaphore_signal(barrier, inc=1, device_id=(bra, lax.rem(ket + step, n_ket)), device_id_type=MESH)
    pl.semaphore_wait(barrier, n_bra + n_ket - 2)

    def hold_copy(step):
        return pltpu.make_async_remote_copy(
            src_ref=dens_ref, dst_ref=held.at[bra], send_sem=hold_send.at[step - 1],
            recv_sem=hold_recv.at[step - 1], device_id=(lax.rem(bra + step, n_bra), ket), device_id_type=MESH)

    for step in range(1, n_bra):
        hold_copy(step).start()
    held[pl.ds(bra, 1)] = dens_ref[...][None]

    live = live_ref[0, 0]
    codes = []
    for t in range(slots):
        code = (tasks_ref[0, 0, t, 0] * blocks + tasks_ref[0, 0, t, 1]) * cols + tasks_ref[0, 0, t, 2] - ket * cols
        codes.append(jnp.where(t < live, code, -1))
    span = blocks * cols

    def count_rows(first, carry):
        rows = lax.broadcasted_iota(jnp.int32, (span, points), 0) + first * span
        total = jnp.zeros((span, points), single)
        for code in codes:
            total += jnp.where(rows == code, 1.0, 0.0)
        counts[pl.ds(pl.multiple_of(first * span, 8), span), :] = total
        return carry

    lax.fori_loop(0, blocks, count_rows, 0)
    for blk in range(blocks):
        factor[blk * width:(blk + 1) * width, :] = fit_ref[blk].astype(single)
    bra_t = jnp.transpose(jnp.concatenate([fit_ref[bra].astype(single), jnp.zeros((lanes - width, points), single)], axis=0)).astype(half)
    ket_f = [fit_ref[ket * cols + d].astype(single) for d in range(cols)]
    pad = -(cols * width) % lanes
    ket_t = jnp.transpose(jnp.concatenate(ket_f + [jnp.zeros((pad, points), single)], axis=0)).astype(half)[:, :cols * width]
    coup_t = jnp.transpose(coup_ref[...])

    for step in range(1, n_bra):
        hold_copy(step).wait_recv()

    for d in range(cols):
        whole = jnp.concatenate([held[blk, d].astype(single) for blk in range(blocks)], axis=0)
        trans[d] = jnp.transpose(whole).astype(half)

    def one_target(s, carry):
        target = lax.rem((ket + 1) * cols + s, blocks)
        fitted = jnp.zeros((dens_count, points), single)
        for d in range(cols):
            mixed = []
            for blk in range(blocks):
                g = factor[blk * width:(blk + 1) * width, :]
                side = counts[pl.ds((blk * blocks + target) * cols + d, 1), :]
                direct = counts[pl.ds((target * blocks + blk) * cols + d, 1), :]
                mixed.append(jnp.concatenate([g * side, g * direct], axis=1))
            weights = jnp.concatenate(mixed, axis=0).astype(half)
            both = jnp.dot(trans[d], weights, preferred_element_type=single)
            for h in range(points // lanes):
                image[d * (points // lanes) + h] = both[:, h * lanes:(h + 1) * lanes]
            cube = both[:, points:].reshape(width, dens_count, points)
            fitted += jnp.sum(cube * ket_f[d][:, None, :], axis=0)
        fit_out[s] = fitted
        g_target = fit_ref[target]
        for k in range(dens_count):
            u_k = jnp.concatenate([
                jnp.concatenate([
                    image[d * (points // lanes) + h, pl.ds(k, width, stride=dens_count), :]
                    for h in range(points // lanes)], axis=1)
                for d in range(cols)], axis=0)
            heavy = jnp.dot(ket_t, u_k.astype(half), preferred_element_type=single)
            wide = (heavy * coup_t).astype(half)
            inner[k * width:(k + 1) * width, :] = jnp.dot(g_target, wide, preferred_element_type=single)
        last = jnp.dot(inner[...].astype(half), bra_t, preferred_element_type=single)
        for k in range(dens_count):
            spread[pl.ds(k, width, stride=dens_count), :] = last[k * width:(k + 1) * width, :]
        term_out[s] = jnp.transpose(spread[...])[:width].astype(half)
        return carry

    def term_copy(s):
        dest = (bra, lax.rem(ket + 1 + s // cols, n_ket))
        return (
            pltpu.make_async_remote_copy(
                src_ref=term_out.at[s], dst_ref=term_in.at[s], send_sem=term_send.at[s],
                recv_sem=term_recv.at[s], device_id=dest, device_id_type=MESH),
            pltpu.make_async_remote_copy(
                src_ref=fit_out.at[s], dst_ref=fit_in.at[s], send_sem=fit_send.at[s],
                recv_sem=fit_recv.at[s], device_id=dest, device_id_type=MESH),
        )

    away = blocks - cols

    def step_body(s, carry):
        one_target(s, 0)

        @pl.when(s < away)
        def _():
            for copy in term_copy(s):
                copy.start()
        return carry

    lax.fori_loop(0, blocks, step_body, 0)

    for s in range(away):
        for copy in term_copy(s):
            copy.wait_recv()
    for y in range(cols):
        exch = term_out[away + y].astype(single)
        fitted = fit_out[away + y]
        for other in range(n_ket - 1):
            exch += term_in[other * cols + y].astype(single)
            fitted += fit_in[other * cols + y]
        exch_ref[y] = exch.astype(half)
        pushed = jnp.dot(fitted, coup_t, precision=lax.Precision.HIGHEST, preferred_element_type=single)
        g_right = fit_ref[ket * cols + y].astype(single)
        rows = (g_right[:, None, :] * pushed[None, :, :]).reshape(flat, points).astype(half)
        out = jnp.dot(rows, bra_t, preferred_element_type=single)
        coul_ref[y] = jnp.transpose(out)[:width].astype(half)

    for step in range(1, n_bra):
        hold_copy(step).wait_send()
    for s in range(away):
        for copy in term_copy(s):
            copy.wait_send()


def per_device(n_bra, n_ket, densities, fit_factors, coupling, quartets, live_count):
    cols, width, flat = densities.shape[1:]
    blocks, points = fit_factors.shape[0], fit_factors.shape[2]
    slots = quartets.shape[2]
    dens_count = flat // width
    dims = (n_bra, n_ket, cols, width, dens_count, points, blocks, slots)
    single, half = jnp.float32, jnp.bfloat16
    away = blocks - cols
    vmem = pl.BlockSpec(memory_space=pltpu.VMEM)
    smem = pl.BlockSpec(memory_space=pltpu.SMEM)
    out = jax.ShapeDtypeStruct((cols, width, flat), half)
    dma = pltpu.SemaphoreType.DMA
    coulomb, exchange = pl.pallas_call(
        functools.partial(kernel, dims),
        out_shape=(out, out),
        in_specs=[smem, smem, vmem, vmem, vmem],
        out_specs=(vmem, vmem),
        scratch_shapes=[
            pltpu.VMEM((n_bra, cols, width, flat), half),
            pltpu.VMEM((blocks * blocks * cols, points), single),
            pltpu.VMEM((blocks * width, points), single),
            pltpu.VMEM((cols, flat, blocks * width), half),
            pltpu.VMEM((cols * (points // 128), flat, 128), single),
            pltpu.VMEM((flat, points), single),
            pltpu.VMEM((flat, 128), single),
            pltpu.VMEM((blocks, width, flat), half),
            pltpu.VMEM((away, width, flat), half),
            pltpu.VMEM((blocks, dens_count, points), single),
            pltpu.VMEM((away, dens_count, points), single),
            dma((n_bra - 1,)), dma((n_bra - 1,)), dma((away,)), dma((away,)), dma((away,)), dma((away,)),
        ],
        compiler_params=pltpu.CompilerParams(collective_id=0, has_side_effects=True, vmem_limit_bytes=56 * 1024 * 1024),
    )(quartets, live_count, densities[0], fit_factors, coupling)
    return coulomb[None], exchange[None]


def solution(mesh):
    placed = (P("bra", "ket", None, None), P(), P(), P("bra", "ket", None, None), P("bra", "ket"))
    return jax.shard_map(
        functools.partial(per_device, mesh.shape["bra"], mesh.shape["ket"]),
        mesh=mesh,
        in_specs=placed,
        out_specs=(P("bra", "ket", None, None), P("bra", "ket", None, None)),
        check_vma=False,
    )
```

```python
import functools

import jax
import jax.numpy as jnp
from jax import lax
from jax.experimental import pallas as pl
from jax.experimental.pallas import tpu as pltpu
from jax.sharding import PartitionSpec as P

MESH = pl.DeviceIdType.MESH


def kernel(dims, tasks_ref, live_ref, dens_ref, fit_ref, coup_ref, coul_ref, exch_ref,
           held, image, stack, fits, wide, inner, spread, term_out, term_in, fit_out, fit_in,
           far_send, far_recv, pair_send, pair_recv, term_send, term_recv, fit_send, fit_recv):
    n_bra, n_ket, cols, width, dens_count, points, blocks, slots, named, padded = dims
    flat = width * dens_count
    lanes = 128
    halves = points // lanes
    single, half = jnp.float32, jnp.bfloat16
    bra, ket = lax.axis_index("bra"), lax.axis_index("ket")
    n_far = n_bra // 2
    far, near = bra // 2, bra % 2
    partner = far * 2 + (1 - near)

    def far_dev(step):
        return (lax.rem(far + step, n_far) * 2 + near, ket)

    def ket_dev(m):
        return (bra, lax.rem(ket + m, n_ket))

    barrier = pltpu.get_barrier_semaphore()
    for step in range(1, n_far):
        pl.semaphore_signal(barrier, inc=1, device_id=far_dev(step), device_id_type=MESH)
    pl.semaphore_signal(barrier, inc=1, device_id=(partner, ket), device_id_type=MESH)
    for m in range(1, n_ket):
        pl.semaphore_signal(barrier, inc=1, device_id=ket_dev(m), device_id_type=MESH)
    pl.semaphore_wait(barrier, n_far + n_ket - 1)

    def far_copy(step):
        return pltpu.make_async_remote_copy(
            src_ref=dens_ref, dst_ref=held.at[bra], send_sem=far_send.at[step - 1],
            recv_sem=far_recv.at[step - 1], device_id=far_dev(step), device_id_type=MESH)

    def column_block(step):
        return lax.rem(far - step + n_far, n_far) * 2

    def pair_copy(step):
        block = column_block(step) + near
        return pltpu.make_async_remote_copy(
            src_ref=held.at[block], dst_ref=held.at[block], send_sem=pair_send.at[step],
            recv_sem=pair_recv.at[step], device_id=(partner, ket), device_id_type=MESH)

    first_copy = pltpu.make_async_remote_copy(
        src_ref=dens_ref, dst_ref=held.at[bra], send_sem=pair_send.at[0],
        recv_sem=pair_recv.at[0], device_id=(partner, ket), device_id_type=MESH)
    first_copy.start()
    for step in range(1, n_far):
        far_copy(step).start()
    held[pl.ds(bra, 1)] = dens_ref[...][None]

    live = live_ref[0, 0]
    rows_b = [tasks_ref[0, 0, t, 0] for t in range(slots)]
    rows_c = [tasks_ref[0, 0, t, 1] for t in range(slots)]
    cols_d = [tasks_ref[0, 0, t, 2] - ket * cols for t in range(slots)]

    def keys_of(rows):
        keys = []
        for t in range(slots):
            rank = jnp.int32(0)
            for before in range(t):
                rank = rank + jnp.where(rows[before] == rows[t], 1, 0)
            keys.append(jnp.where(t < live, rows[t] * named + rank, -1))
        return keys

    keys_b, keys_c = keys_of(rows_b), keys_of(rows_c)
    pairs_b = [rows_b[t] * cols + cols_d[t] + 1 for t in range(slots)]
    pairs_c = [rows_c[t] * cols + cols_d[t] + 1 for t in range(slots)]

    def find(keys, values, want):
        found = jnp.int32(0)
        for t in range(slots):
            found = found + jnp.where(keys[t] == want, values[t], 0)
        return jnp.maximum(found - 1, 0), jnp.where(found > 0, 1.0, 0.0)

    bra_t = jnp.transpose(jnp.concatenate([fit_ref[bra].astype(single), jnp.zeros((lanes - width, points), single)], axis=0)).astype(half)
    ket_f = [fit_ref[ket * cols + d].astype(single) for d in range(cols)]
    coup_t = jnp.transpose(coup_ref[...])

    def process(block):
        for d in range(cols):
            both = lax.dot_general(held[block, d], fit_ref[block], (((0,), (0,)), ((), ())), preferred_element_type=single)
            fits[block * cols + d] = jnp.sum(both.reshape(width, dens_count, points) * ket_f[d][:, None, :], axis=0)
            for h in range(halves):
                image[d * halves + h] = both[:, h * lanes:(h + 1) * lanes]
            for k in range(dens_count):
                part = jnp.concatenate([image[d * halves + h, pl.ds(k, width, stride=dens_count), :] for h in range(halves)], axis=1)
                part = jnp.concatenate([part, jnp.zeros((padded - width, points), single)], axis=0)
                stack[block * cols + d, k] = part.astype(half)

    def gather_step(step, carry):
        @pl.when(step > 0)
        def _():
            far_copy(step).wait_recv()
            pair_copy(step).start()
        process(column_block(step) + near)

        @pl.when(step > 0)
        def _():
            pair_copy(step - 1).wait_recv()
            process(column_block(step - 1) + 1 - near)
        return carry

    lax.fori_loop(0, n_far, gather_step, 0)
    pair_copy(n_far - 1).wait_recv()
    process(column_block(n_far - 1) + 1 - near)

    def holder_of(m):
        return lax.rem(ket + m, n_ket)

    def fit_copy(m):
        return pltpu.make_async_remote_copy(
            src_ref=fit_out.at[m], dst_ref=fit_in.at[m - 1], send_sem=fit_send.at[m - 1],
            recv_sem=fit_recv.at[m - 1], device_id=ket_dev(m), device_id_type=MESH)

    def fit_target(s, carry):
        target = holder_of(1 + s // cols) * cols + s % cols
        total = jnp.zeros((dens_count, points), single)
        for n in range(named):
            at, scale = find(keys_b, pairs_c, target * named + n)
            total += fits[at] * scale
        fit_out[lax.rem(1 + s // cols, n_ket), s % cols] = total
        return carry

    lax.fori_loop(0, blocks, fit_target, 0)
    for m in range(1, n_ket):
        fit_copy(m).start()

    def one_target(s):
        target = holder_of(1 + s // cols) * cols + s % cols
        found = [find(keys_c, pairs_b, target * named + n) for n in range(named)]
        right = []
        for at, scale in found:
            right.append(fit_ref[ket * cols + lax.rem(at, cols)].astype(single) * scale)
            right.append(jnp.zeros((padded - width, points), single))
        depth = named * padded
        right.append(jnp.zeros((-depth % lanes, points), single))
        right_t = jnp.transpose(jnp.concatenate(right, axis=0)).astype(half)[:, :depth]
        for k in range(dens_count):
            left = jnp.concatenate([stack[at, k] for at, _ in found], axis=0)
            heavy = jnp.dot(right_t, left, preferred_element_type=single)
            wide[:, k * points:(k + 1) * points] = (heavy * coup_t).astype(half)
        g_target = fit_ref[target]
        for k in range(dens_count):
            inner[k * width:(k + 1) * width, :] = jnp.dot(
                g_target, wide[:, k * points:(k + 1) * points], preferred_element_type=single)
        last = jnp.dot(inner[...].astype(half), bra_t, preferred_element_type=single)
        for k in range(dens_count):
            spread[pl.ds(k, width, stride=dens_count), :] = last[k * width:(k + 1) * width, :]
        term_out[s] = jnp.transpose(spread[...])[:width].astype(half)

    def term_copy(s):
        return pltpu.make_async_remote_copy(
            src_ref=term_out.at[s], dst_ref=term_in.at[s], send_sem=term_send.at[s],
            recv_sem=term_recv.at[s], device_id=ket_dev(1 + s // cols), device_id_type=MESH)

    away = blocks - cols

    def step_body(s, carry):
        one_target(s)

        @pl.when(s < away)
        def _():
            term_copy(s).start()
        return carry

    lax.fori_loop(0, blocks, step_body, 0)

    for m in range(1, n_ket):
        fit_copy(m).wait_recv()
    for y in range(cols):
        fitted = fit_out[0, y]
        for other in range(n_ket - 1):
            fitted += fit_in[other, y]
        pushed = jnp.dot(fitted, coup_t, precision=lax.Precision.HIGHEST, preferred_element_type=single)
        g_right = fit_ref[ket * cols + y].astype(single)
        rows = (g_right[:, None, :] * pushed[None, :, :]).reshape(flat, points).astype(half)
        out = jnp.dot(rows, bra_t, preferred_element_type=single)
        coul_ref[y] = jnp.transpose(out)[:width].astype(half)
    for s in range(away):
        term_copy(s).wait_recv()
    for y in range(cols):
        exch = term_out[away + y].astype(single)
        for other in range(n_ket - 1):
            exch += term_in[other * cols + y].astype(single)
        exch_ref[y] = exch.astype(half)

    for step in range(1, n_far):
        far_copy(step).wait_send()
    first_copy.wait_send()
    for step in range(1, n_far):
        pair_copy(step).wait_send()
    for m in range(1, n_ket):
        fit_copy(m).wait_send()
    for s in range(away):
        term_copy(s).wait_send()


def per_device(n_bra, n_ket, densities, fit_factors, coupling, quartets, live_count):
    cols, width, flat = densities.shape[1:]
    blocks, points = fit_factors.shape[0], fit_factors.shape[2]
    slots = quartets.shape[2]
    dens_count = flat // width
    named = 2 * slots // blocks
    padded = -(-width // 16) * 16
    dims = (n_bra, n_ket, cols, width, dens_count, points, blocks, slots, named, padded)
    single, half = jnp.float32, jnp.bfloat16
    away = blocks - cols
    vmem = pl.BlockSpec(memory_space=pltpu.VMEM)
    smem = pl.BlockSpec(memory_space=pltpu.SMEM)
    out = jax.ShapeDtypeStruct((cols, width, flat), half)
    dma = pltpu.SemaphoreType.DMA
    coulomb, exchange = pl.pallas_call(
        functools.partial(kernel, dims),
        out_shape=(out, out),
        in_specs=[smem, smem, vmem, vmem, vmem],
        out_specs=(vmem, vmem),
        scratch_shapes=[
            pltpu.VMEM((n_bra, cols, width, flat), half),
            pltpu.VMEM((cols * (points // 128), flat, 128), single),
            pltpu.VMEM((blocks * cols, dens_count, padded, points), half),
            pltpu.VMEM((blocks * cols, dens_count, points), single),
            pltpu.VMEM((points, dens_count * points), half),
            pltpu.VMEM((flat, points), single),
            pltpu.VMEM((flat, 128), single),
            pltpu.VMEM((blocks, width, flat), half),
            pltpu.VMEM((away, width, flat), half),
            pltpu.VMEM((n_ket, cols, dens_count, points), single),
            pltpu.VMEM((n_ket - 1, cols, dens_count, points), single),
            dma((n_bra // 2 - 1,)), dma((n_bra // 2 - 1,)), dma((n_bra // 2,)), dma((n_bra // 2,)),
            dma((away,)), dma((away,)), dma((n_ket - 1,)), dma((n_ket - 1,)),
        ],
        compiler_params=pltpu.CompilerParams(collective_id=0, has_side_effects=True, vmem_limit_bytes=56 * 1024 * 1024),
    )(quartets, live_count, densities[0], fit_factors, coupling)
    return coulomb[None], exchange[None]


def solution(mesh):
    placed = (P("bra", "ket", None, None), P(), P(), P("bra", "ket", None, None), P("bra", "ket"))
    return jax.shard_map(
        functools.partial(per_device, mesh.shape["bra"], mesh.shape["ket"]),
        mesh=mesh,
        in_specs=placed,
        out_specs=(P("bra", "ket", None, None), P("bra", "ket", None, None)),
        check_vma=False,
    )
```

```python
import functools

import jax
import jax.numpy as jnp
from jax import lax
from jax.experimental import pallas as pl
from jax.experimental.pallas import tpu as pltpu
from jax.sharding import PartitionSpec as P

MESH = pl.DeviceIdType.MESH


def kernel(dims, tasks_ref, live_ref, dens_ref, fit_ref, coup_ref, coul_ref, exch_ref,
           held, image, stack, fits, wide, inner, spread, term_out, term_in, fit_out, fit_in,
           right_all, pick_b, pick_c, gain_b,
           up_send, up_recv, down_send, down_recv, pair_send, pair_recv, term_send, term_recv, fit_send, fit_recv):
    n_bra, n_ket, cols, width, dens_count, points, blocks, slots, named, padded = dims
    flat = width * dens_count
    lanes = 128
    halves = points // lanes
    single, half = jnp.float32, jnp.bfloat16
    bra, ket = lax.axis_index("bra"), lax.axis_index("ket")
    n_far = n_bra // 2
    far, near = bra // 2, bra % 2
    partner = far * 2 + (1 - near)

    def ket_dev(m):
        return (bra, lax.rem(ket + m, n_ket))

    barrier = pltpu.get_barrier_semaphore()
    has_up, has_down = far + 1 < n_far, far > 0

    @pl.when(has_up)
    def _():
        pl.semaphore_signal(barrier, inc=1, device_id=(bra + 2, ket), device_id_type=MESH)

    @pl.when(has_down)
    def _():
        pl.semaphore_signal(barrier, inc=1, device_id=(bra - 2, ket), device_id_type=MESH)

    pl.semaphore_signal(barrier, inc=1, device_id=(partner, ket), device_id_type=MESH)
    for m in range(1, n_ket):
        pl.semaphore_signal(barrier, inc=1, device_id=ket_dev(m), device_id_type=MESH)
    pl.semaphore_wait(barrier, n_ket + jnp.minimum(n_far - 1 - far, 1) + jnp.minimum(far, 1))

    def up_copy(dist, src=None):
        block = bra - 2 * dist
        return pltpu.make_async_remote_copy(
            src_ref=held.at[block] if src is None else src, dst_ref=held.at[block], send_sem=up_send.at[dist],
            recv_sem=up_recv.at[dist], device_id=(bra + 2, ket), device_id_type=MESH)

    def down_copy(dist, src=None):
        block = bra + 2 * dist
        return pltpu.make_async_remote_copy(
            src_ref=held.at[block] if src is None else src, dst_ref=held.at[block], send_sem=down_send.at[dist],
            recv_sem=down_recv.at[dist], device_id=(bra - 2, ket), device_id_type=MESH)

    def pair_copy(row):
        block = row * 2 + near
        return pltpu.make_async_remote_copy(
            src_ref=held.at[block], dst_ref=held.at[block], send_sem=pair_send.at[row],
            recv_sem=pair_recv.at[row], device_id=(partner, ket), device_id_type=MESH)

    def pair_wait(row):
        block = row * 2 + 1 - near
        pltpu.make_async_remote_copy(
            src_ref=held.at[block], dst_ref=held.at[block], send_sem=pair_send.at[row],
            recv_sem=pair_recv.at[row], device_id=(partner, ket), device_id_type=MESH).wait_recv()

    def up_wait(dist):
        block = bra - 2 * dist
        pltpu.make_async_remote_copy(
            src_ref=held.at[block], dst_ref=held.at[block], send_sem=up_send.at[dist - 1],
            recv_sem=up_recv.at[dist - 1], device_id=(bra - 2, ket), device_id_type=MESH).wait_recv()

    def down_wait(dist):
        block = bra + 2 * dist
        pltpu.make_async_remote_copy(
            src_ref=held.at[block], dst_ref=held.at[block], send_sem=down_send.at[dist - 1],
            recv_sem=down_recv.at[dist - 1], device_id=(bra + 2, ket), device_id_type=MESH).wait_recv()

    first_copy = pltpu.make_async_remote_copy(
        src_ref=dens_ref, dst_ref=held.at[bra], send_sem=pair_send.at[far],
        recv_sem=pair_recv.at[far], device_id=(partner, ket), device_id_type=MESH)
    first_copy.start()

    @pl.when(has_up)
    def _():
        up_copy(0, dens_ref).start()

    @pl.when(has_down)
    def _():
        down_copy(0, dens_ref).start()

    held[pl.ds(bra, 1)] = dens_ref[...][None]

    live = live_ref[0, 0]
    rows_b = [tasks_ref[0, 0, 0, t] for t in range(slots)]
    rows_c = [tasks_ref[0, 1, 0, t] for t in range(slots)]
    cols_d = [tasks_ref[0, 2, 0, t] - ket * cols for t in range(slots)]

    def keys_of(rows):
        keys = []
        for t in range(slots):
            rank = jnp.int32(0)
            for before in range(t):
                rank = rank + jnp.where(rows[before] == rows[t], 1, 0)
            keys.append(jnp.where(t < live, rows[t] * named + rank, -1))
        return keys

    keys_b, keys_c = keys_of(rows_b), keys_of(rows_c)
    pairs_b = [rows_b[t] * cols + cols_d[t] + 1 for t in range(slots)]
    pairs_c = [rows_c[t] * cols + cols_d[t] + 1 for t in range(slots)]

    def find(keys, values, want):
        found = jnp.int32(0)
        for t in range(slots):
            found = found + jnp.where(keys[t] == want, values[t], 0)
        return jnp.maximum(found - 1, 0), jnp.where(found > 0, 1.0, 0.0)

    bra_t = jnp.transpose(jnp.concatenate([fit_ref[bra].astype(single), jnp.zeros((lanes - width, points), single)], axis=0)).astype(half)
    ket_f = [fit_ref[ket * cols + d].astype(single) for d in range(cols)]
    coup_t = jnp.transpose(coup_ref[...])

    def holder_of(m):
        return lax.rem(ket + m, n_ket)

    depth = named * padded

    def list_target(s, carry):
        target = holder_of(1 + s // cols) * cols + s % cols
        right = []
        for n in range(named):
            at, scale = find(keys_b, pairs_c, target * named + n)
            pick_b[s, n] = at
            gain_b[s, n] = scale
            at, scale = find(keys_c, pairs_b, target * named + n)
            pick_c[s, n] = at
            right.append(fit_ref[ket * cols + lax.rem(at, cols)].astype(single) * scale)
            right.append(jnp.zeros((padded - width, points), single))
        right.append(jnp.zeros((-depth % lanes, points), single))
        right_all[s] = jnp.transpose(jnp.concatenate(right, axis=0)).astype(half)
        return carry

    def process(block):
        for d in range(cols):
            both = lax.dot_general(held[block, d], fit_ref[block], (((0,), (0,)), ((), ())), preferred_element_type=single)
            fits[block * cols + d] = jnp.sum(both.reshape(width, dens_count, points) * ket_f[d][:, None, :], axis=0)
            for h in range(halves):
                image[d * halves + h] = both[:, h * lanes:(h + 1) * lanes]
            for k in range(dens_count):
                part = jnp.concatenate([image[d * halves + h, pl.ds(k, width, stride=dens_count), :] for h in range(halves)], axis=1)
                part = jnp.concatenate([part, jnp.zeros((padded - width, points), single)], axis=0)
                stack[block * cols + d, k] = part.astype(half)

    lax.fori_loop(0, blocks, list_target, 0)

    def gather_step(dist, carry):
        below, above = far - dist, far + dist

        @pl.when(below >= 0)
        def _():
            @pl.when(dist > 0)
            def _():
                up_wait(dist)
                pair_copy(below).start()

                @pl.when(has_up)
                def _():
                    up_copy(dist).start()

        @pl.when((above < n_far) & (dist > 0))
        def _():
            down_wait(dist)
            pair_copy(above).start()

            @pl.when(has_down)
            def _():
                down_copy(dist).start()

        @pl.when(below >= 0)
        def _():
            process(below * 2 + near)
            pair_wait(below)
            process(below * 2 + 1 - near)

        @pl.when((above < n_far) & (dist > 0))
        def _():
            process(above * 2 + near)
            pair_wait(above)
            process(above * 2 + 1 - near)
        return carry

    lax.fori_loop(0, n_far, gather_step, 0)

    def fit_copy(m):
        return pltpu.make_async_remote_copy(
            src_ref=fit_out.at[m], dst_ref=fit_in.at[m - 1], send_sem=fit_send.at[m - 1],
            recv_sem=fit_recv.at[m - 1], device_id=ket_dev(m), device_id_type=MESH)

    def fit_target(s, carry):
        total = jnp.zeros((dens_count, points), single)
        for n in range(named):
            total += fits[pick_b[s, n]] * gain_b[s, n]
        fit_out[lax.rem(1 + s // cols, n_ket), s % cols] = total
        return carry

    lax.fori_loop(0, blocks, fit_target, 0)
    for m in range(1, n_ket):
        fit_copy(m).start()

    def one_target(s):
        target = holder_of(1 + s // cols) * cols + s % cols
        found = [pick_c[s, n] for n in range(named)]
        right_t = right_all[s][:, :depth]
        for k in range(dens_count):
            left = jnp.concatenate([stack[at, k] for at in found], axis=0)
            heavy = jnp.dot(right_t, left, preferred_element_type=single)
            wide[:, k * points:(k + 1) * points] = (heavy * coup_t).astype(half)
        g_target = fit_ref[target]
        for k in range(dens_count):
            inner[k * width:(k + 1) * width, :] = jnp.dot(
                g_target, wide[:, k * points:(k + 1) * points], preferred_element_type=single)
        last = jnp.dot(inner[...].astype(half), bra_t, preferred_element_type=single)
        for k in range(dens_count):
            spread[pl.ds(k, width, stride=dens_count), :] = last[k * width:(k + 1) * width, :]
        term_out[s] = jnp.transpose(spread[...])[:width].astype(half)

    def term_copy(s):
        return pltpu.make_async_remote_copy(
            src_ref=term_out.at[s], dst_ref=term_in.at[s], send_sem=term_send.at[s],
            recv_sem=term_recv.at[s], device_id=ket_dev(1 + s // cols), device_id_type=MESH)

    away = blocks - cols

    def step_body(s, carry):
        one_target(s)

        @pl.when(s < away)
        def _():
            term_copy(s).start()
        return carry

    lax.fori_loop(0, blocks, step_body, 0)

    for m in range(1, n_ket):
        fit_copy(m).wait_recv()
    for y in range(cols):
        fitted = fit_out[0, y]
        for other in range(n_ket - 1):
            fitted += fit_in[other, y]
        pushed = jnp.dot(fitted, coup_t, precision=lax.Precision.HIGHEST, preferred_element_type=single)
        g_right = fit_ref[ket * cols + y].astype(single)
        rows = (g_right[:, None, :] * pushed[None, :, :]).reshape(flat, points).astype(half)
        out = jnp.dot(rows, bra_t, preferred_element_type=single)
        coul_ref[y] = jnp.transpose(out)[:width].astype(half)
    for s in range(away):
        term_copy(s).wait_recv()
    for y in range(cols):
        exch = term_out[away + y].astype(single)
        for other in range(n_ket - 1):
            exch += term_in[other * cols + y].astype(single)
        exch_ref[y] = exch.astype(half)

    first_copy.wait_send()

    def drain(dist, carry):
        @pl.when((far - dist >= 0) & has_up)
        def _():
            up_copy(dist).wait_send()

        @pl.when((far + dist < n_far) & has_down)
        def _():
            down_copy(dist).wait_send()

        @pl.when((far - dist >= 0) & (dist > 0))
        def _():
            pair_copy(far - dist).wait_send()

        @pl.when((far + dist < n_far) & (dist > 0))
        def _():
            pair_copy(far + dist).wait_send()
        return carry

    lax.fori_loop(0, n_far, drain, 0)
    for m in range(1, n_ket):
        fit_copy(m).wait_send()
    for s in range(away):
        term_copy(s).wait_send()


def per_device(n_bra, n_ket, densities, fit_factors, coupling, quartets, live_count):
    cols, width, flat = densities.shape[1:]
    blocks, points = fit_factors.shape[0], fit_factors.shape[2]
    slots = quartets.shape[2]
    dens_count = flat // width
    named = 2 * slots // blocks
    padded = -(-width // 16) * 16
    dims = (n_bra, n_ket, cols, width, dens_count, points, blocks, slots, named, padded)
    single, half = jnp.float32, jnp.bfloat16
    away = blocks - cols
    vmem = pl.BlockSpec(memory_space=pltpu.VMEM)
    smem = pl.BlockSpec(memory_space=pltpu.SMEM)
    out = jax.ShapeDtypeStruct((cols, width, flat), half)
    dma = pltpu.SemaphoreType.DMA
    coulomb, exchange = pl.pallas_call(
        functools.partial(kernel, dims),
        out_shape=(out, out),
        in_specs=[smem, smem, vmem, vmem, vmem],
        out_specs=(vmem, vmem),
        scratch_shapes=[
            pltpu.VMEM((n_bra, cols, width, flat), half),
            pltpu.VMEM((cols * (points // 128), flat, 128), single),
            pltpu.VMEM((blocks * cols, dens_count, padded, points), half),
            pltpu.VMEM((blocks * cols, dens_count, points), single),
            pltpu.VMEM((points, dens_count * points), half),
            pltpu.VMEM((flat, points), single),
            pltpu.VMEM((flat, 128), single),
            pltpu.VMEM((blocks, width, flat), half),
            pltpu.VMEM((away, width, flat), half),
            pltpu.VMEM((n_ket, cols, dens_count, points), single),
            pltpu.VMEM((n_ket - 1, cols, dens_count, points), single),
            pltpu.VMEM((blocks, points, -(-named * padded // 128) * 128), half),
            pltpu.SMEM((blocks, named), jnp.int32),
            pltpu.SMEM((blocks, named), jnp.int32),
            pltpu.SMEM((blocks, named), single),
            dma((n_bra // 2,)), dma((n_bra // 2,)), dma((n_bra // 2,)), dma((n_bra // 2,)),
            dma((n_bra // 2,)), dma((n_bra // 2,)),
            dma((away,)), dma((away,)), dma((n_ket - 1,)), dma((n_ket - 1,)),
        ],
        compiler_params=pltpu.CompilerParams(collective_id=0, has_side_effects=True, vmem_limit_bytes=56 * 1024 * 1024),
    )(jnp.transpose(quartets, (0, 3, 1, 2)), live_count, densities[0], fit_factors, coupling)
    return coulomb[None], exchange[None]


def solution(mesh):
    placed = (P("bra", "ket", None, None), P(), P(), P("bra", "ket", None, None), P("bra", "ket"))
    return jax.shard_map(
        functools.partial(per_device, mesh.shape["bra"], mesh.shape["ket"]),
        mesh=mesh,
        in_specs=placed,
        out_specs=(P("bra", "ket", None, None), P("bra", "ket", None, None)),
        check_vma=False,
    )
```

```python
import functools

import jax
import jax.numpy as jnp
from jax import lax
from jax.experimental import pallas as pl
from jax.experimental.pallas import tpu as pltpu
from jax.sharding import PartitionSpec as P

MESH = pl.DeviceIdType.MESH


def kernel(dims, tasks_ref, live_ref, dens_ref, fit_ref, coup_ref, coul_ref, exch_ref,
           held, image, stack, fits, wide, inner, spread, term_out, term_in, fit_out, fit_in,
           right_all, pick_b, pick_c, gain_b,
           far_send, far_recv, pair_send, pair_recv, term_send, term_recv, fit_send, fit_recv):
    n_bra, n_ket, cols, width, dens_count, points, blocks, slots, named, padded = dims
    flat = width * dens_count
    lanes = 128
    halves = points // lanes
    single, half = jnp.float32, jnp.bfloat16
    bra, ket = lax.axis_index("bra"), lax.axis_index("ket")
    n_far = n_bra // 2
    far, near = bra // 2, bra % 2
    partner = far * 2 + (1 - near)

    def far_dev(step):
        return (lax.rem(far + step, n_far) * 2 + near, ket)

    def ket_dev(m):
        return (bra, lax.rem(ket + m, n_ket))

    barrier = pltpu.get_barrier_semaphore()
    for step in range(1, n_far):
        pl.semaphore_signal(barrier, inc=1, device_id=far_dev(step), device_id_type=MESH)
    pl.semaphore_signal(barrier, inc=1, device_id=(partner, ket), device_id_type=MESH)
    for m in range(1, n_ket):
        pl.semaphore_signal(barrier, inc=1, device_id=ket_dev(m), device_id_type=MESH)
    pl.semaphore_wait(barrier, n_far + n_ket - 1)

    def order(at):
        if isinstance(at, int):
            return (at + 1) // 2 if at % 2 else (n_far - at // 2) % n_far
        return jnp.where(at % 2 == 1, (at + 1) // 2, (n_far - at // 2) % n_far)

    def far_copy(step):
        return pltpu.make_async_remote_copy(
            src_ref=dens_ref, dst_ref=held.at[bra], send_sem=far_send.at[step - 1],
            recv_sem=far_recv.at[step - 1], device_id=far_dev(step), device_id_type=MESH)

    def column_block(step):
        return lax.rem(far - step + n_far, n_far) * 2

    def pair_copy(step):
        block = column_block(step) + near
        return pltpu.make_async_remote_copy(
            src_ref=held.at[block], dst_ref=held.at[block], send_sem=pair_send.at[step],
            recv_sem=pair_recv.at[step], device_id=(partner, ket), device_id_type=MESH)

    first_copy = pltpu.make_async_remote_copy(
        src_ref=dens_ref, dst_ref=held.at[bra], send_sem=pair_send.at[0],
        recv_sem=pair_recv.at[0], device_id=(partner, ket), device_id_type=MESH)
    first_copy.start()

    for step in [order(at) for at in range(1, n_far)]:
        far_copy(step).start()
    held[pl.ds(bra, 1)] = dens_ref[...][None]

    live = live_ref[0, 0]
    rows_b = [tasks_ref[0, 0, 0, t] for t in range(slots)]
    rows_c = [tasks_ref[0, 1, 0, t] for t in range(slots)]
    cols_d = [tasks_ref[0, 2, 0, t] - ket * cols for t in range(slots)]

    def keys_of(rows):
        keys = []
        for t in range(slots):
            rank = jnp.int32(0)
            for before in range(t):
                rank = rank + jnp.where(rows[before] == rows[t], 1, 0)
            keys.append(jnp.where(t < live, rows[t] * named + rank, -1))
        return keys

    keys_b, keys_c = keys_of(rows_b), keys_of(rows_c)
    pairs_b = [rows_b[t] * cols + cols_d[t] + 1 for t in range(slots)]
    pairs_c = [rows_c[t] * cols + cols_d[t] + 1 for t in range(slots)]

    def find(keys, values, want):
        found = jnp.int32(0)
        for t in range(slots):
            found = found + jnp.where(keys[t] == want, values[t], 0)
        return jnp.maximum(found - 1, 0), jnp.where(found > 0, 1.0, 0.0)

    bra_t = jnp.transpose(jnp.concatenate([fit_ref[bra].astype(single), jnp.zeros((lanes - width, points), single)], axis=0)).astype(half)
    ket_f = [fit_ref[ket * cols + d].astype(single) for d in range(cols)]
    coup_t = jnp.transpose(coup_ref[...])

    def holder_of(m):
        return lax.rem(ket + m, n_ket)

    depth = named * padded

    def list_target(s, carry):
        target = holder_of(1 + s // cols) * cols + s % cols
        right = []
        for n in range(named):
            at, scale = find(keys_b, pairs_c, target * named + n)
            pick_b[s, n] = at
            gain_b[s, n] = scale
            at, scale = find(keys_c, pairs_b, target * named + n)
            pick_c[s, n] = at
            right.append(fit_ref[ket * cols + lax.rem(at, cols)].astype(single) * scale)
            right.append(jnp.zeros((padded - width, points), single))
        right.append(jnp.zeros((-depth % lanes, points), single))
        right_all[s] = jnp.transpose(jnp.concatenate(right, axis=0)).astype(half)
        return carry

    def process(block):
        for d in range(cols):
            both = lax.dot_general(held[block, d], fit_ref[block], (((0,), (0,)), ((), ())), preferred_element_type=single)
            fits[block * cols + d] = jnp.sum(both.reshape(width, dens_count, points) * ket_f[d][:, None, :], axis=0)
            for h in range(halves):
                image[d * halves + h] = both[:, h * lanes:(h + 1) * lanes]
            for k in range(dens_count):
                part = jnp.concatenate([image[d * halves + h, pl.ds(k, width, stride=dens_count), :] for h in range(halves)], axis=1)
                part = jnp.concatenate([part, jnp.zeros((padded - width, points), single)], axis=0)
                stack[block * cols + d, k] = part.astype(half)

    lax.fori_loop(0, blocks, list_target, 0)

    def gather_step(at, carry):
        step = order(at)

        @pl.when(at > 0)
        def _():
            far_copy(step).wait_recv()
            pair_copy(step).start()
        process(column_block(step) + near)

        @pl.when(at > 0)
        def _():
            past = order(at - 1)
            pair_copy(past).wait_recv()
            process(column_block(past) + 1 - near)
        return carry

    lax.fori_loop(0, n_far, gather_step, 0)
    pair_copy(order(n_far - 1)).wait_recv()
    process(column_block(order(n_far - 1)) + 1 - near)

    def fit_copy(m):
        return pltpu.make_async_remote_copy(
            src_ref=fit_out.at[m], dst_ref=fit_in.at[m - 1], send_sem=fit_send.at[m - 1],
            recv_sem=fit_recv.at[m - 1], device_id=ket_dev(m), device_id_type=MESH)

    def fit_target(s, carry):
        total = jnp.zeros((dens_count, points), single)
        for n in range(named):
            total += fits[pick_b[s, n]] * gain_b[s, n]
        fit_out[lax.rem(1 + s // cols, n_ket), s % cols] = total
        return carry

    lax.fori_loop(0, blocks, fit_target, 0)
    for m in range(1, n_ket):
        fit_copy(m).start()

    def one_target(s):
        target = holder_of(1 + s // cols) * cols + s % cols
        found = [pick_c[s, n] for n in range(named)]
        right_t = right_all[s][:, :depth]
        for k in range(dens_count):
            left = jnp.concatenate([stack[at, k] for at in found], axis=0)
            heavy = jnp.dot(right_t, left, preferred_element_type=single)
            wide[:, k * points:(k + 1) * points] = (heavy * coup_t).astype(half)
        g_target = fit_ref[target]
        for k in range(dens_count):
            inner[k * width:(k + 1) * width, :] = jnp.dot(
                g_target, wide[:, k * points:(k + 1) * points], preferred_element_type=single)
        last = jnp.dot(inner[...].astype(half), bra_t, preferred_element_type=single)
        for k in range(dens_count):
            spread[pl.ds(k, width, stride=dens_count), :] = last[k * width:(k + 1) * width, :]
        term_out[s] = jnp.transpose(spread[...])[:width].astype(half)

    def term_copy(s):
        return pltpu.make_async_remote_copy(
            src_ref=term_out.at[s], dst_ref=term_in.at[s], send_sem=term_send.at[s],
            recv_sem=term_recv.at[s], device_id=ket_dev(1 + s // cols), device_id_type=MESH)

    away = blocks - cols

    def step_body(s, carry):
        one_target(s)

        @pl.when(s < away)
        def _():
            term_copy(s).start()
        return carry

    lax.fori_loop(0, blocks, step_body, 0)

    for m in range(1, n_ket):
        fit_copy(m).wait_recv()
    for y in range(cols):
        fitted = fit_out[0, y]
        for other in range(n_ket - 1):
            fitted += fit_in[other, y]
        pushed = jnp.dot(fitted, coup_t, precision=lax.Precision.HIGHEST, preferred_element_type=single)
        g_right = fit_ref[ket * cols + y].astype(single)
        rows = (g_right[:, None, :] * pushed[None, :, :]).reshape(flat, points).astype(half)
        out = jnp.dot(rows, bra_t, preferred_element_type=single)
        coul_ref[y] = jnp.transpose(out)[:width].astype(half)
    for s in range(away):
        term_copy(s).wait_recv()
    for y in range(cols):
        exch = term_out[away + y].astype(single)
        for other in range(n_ket - 1):
            exch += term_in[other * cols + y].astype(single)
        exch_ref[y] = exch.astype(half)

    for step in range(1, n_far):
        far_copy(step).wait_send()
    first_copy.wait_send()
    for step in range(1, n_far):
        pair_copy(step).wait_send()
    for m in range(1, n_ket):
        fit_copy(m).wait_send()
    for s in range(away):
        term_copy(s).wait_send()


def per_device(n_bra, n_ket, densities, fit_factors, coupling, quartets, live_count):
    cols, width, flat = densities.shape[1:]
    blocks, points = fit_factors.shape[0], fit_factors.shape[2]
    slots = quartets.shape[2]
    dens_count = flat // width
    named = 2 * slots // blocks
    padded = -(-width // 16) * 16
    dims = (n_bra, n_ket, cols, width, dens_count, points, blocks, slots, named, padded)
    single, half = jnp.float32, jnp.bfloat16
    away = blocks - cols
    vmem = pl.BlockSpec(memory_space=pltpu.VMEM)
    smem = pl.BlockSpec(memory_space=pltpu.SMEM)
    out = jax.ShapeDtypeStruct((cols, width, flat), half)
    dma = pltpu.SemaphoreType.DMA
    coulomb, exchange = pl.pallas_call(
        functools.partial(kernel, dims),
        out_shape=(out, out),
        in_specs=[smem, smem, vmem, vmem, vmem],
        out_specs=(vmem, vmem),
        scratch_shapes=[
            pltpu.VMEM((n_bra, cols, width, flat), half),
            pltpu.VMEM((cols * (points // 128), flat, 128), single),
            pltpu.VMEM((blocks * cols, dens_count, padded, points), half),
            pltpu.VMEM((blocks * cols, dens_count, points), single),
            pltpu.VMEM((points, dens_count * points), half),
            pltpu.VMEM((flat, points), single),
            pltpu.VMEM((flat, 128), single),
            pltpu.VMEM((blocks, width, flat), half),
            pltpu.VMEM((away, width, flat), half),
            pltpu.VMEM((n_ket, cols, dens_count, points), single),
            pltpu.VMEM((n_ket - 1, cols, dens_count, points), single),
            pltpu.VMEM((blocks, points, -(-named * padded // 128) * 128), half),
            pltpu.SMEM((blocks, named), jnp.int32),
            pltpu.SMEM((blocks, named), jnp.int32),
            pltpu.SMEM((blocks, named), single),
            dma((n_bra // 2 - 1,)), dma((n_bra // 2 - 1,)), dma((n_bra // 2,)), dma((n_bra // 2,)),
            dma((away,)), dma((away,)), dma((n_ket - 1,)), dma((n_ket - 1,)),
        ],
        compiler_params=pltpu.CompilerParams(collective_id=0, has_side_effects=True, vmem_limit_bytes=56 * 1024 * 1024),
    )(jnp.transpose(quartets, (0, 3, 1, 2)), live_count, densities[0], fit_factors, coupling)
    return coulomb[None], exchange[None]


def solution(mesh):
    placed = (P("bra", "ket", None, None), P(), P(), P("bra", "ket", None, None), P("bra", "ket"))
    return jax.shard_map(
        functools.partial(per_device, mesh.shape["bra"], mesh.shape["ket"]),
        mesh=mesh,
        in_specs=placed,
        out_specs=(P("bra", "ket", None, None), P("bra", "ket", None, None)),
        check_vma=False,
    )
```

```python
import functools

import jax
import jax.numpy as jnp
from jax import lax
from jax.experimental import pallas as pl
from jax.experimental.pallas import tpu as pltpu
from jax.sharding import PartitionSpec as P

MESH = pl.DeviceIdType.MESH


def kernel(dims, tasks_ref, live_ref, dens_ref, fit_hbm, coup_hbm, coul_ref, exch_ref,
           held, image, stack, fits, wide, inner, spread, term_out, term_in, fit_out, fit_in,
           fit_ref, coup_ref, load_sem, right_all, pick_b, pick_c, gain_b,
           far_send, far_recv, pair_send, pair_recv, term_send, term_recv, fit_send, fit_recv):
    n_bra, n_ket, cols, width, dens_count, points, blocks, slots, named, padded = dims
    flat = width * dens_count
    lanes = 128
    halves = points // lanes
    single, half = jnp.float32, jnp.bfloat16
    bra, ket = lax.axis_index("bra"), lax.axis_index("ket")
    n_far = n_bra // 2
    far, near = bra // 2, bra % 2
    partner = far * 2 + (1 - near)

    def far_dev(step):
        return (lax.rem(far + step, n_far) * 2 + near, ket)

    def ket_dev(m):
        return (bra, lax.rem(ket + m, n_ket))

    loads = (
        pltpu.make_async_copy(dens_ref, held.at[bra], load_sem.at[0]),
        pltpu.make_async_copy(fit_hbm, fit_ref, load_sem.at[1]),
        pltpu.make_async_copy(coup_hbm, coup_ref, load_sem.at[2]),
    )
    for load in loads:
        load.start()
    barrier = pltpu.get_barrier_semaphore()
    for step in range(1, n_far):
        pl.semaphore_signal(barrier, inc=1, device_id=far_dev(step), device_id_type=MESH)
    pl.semaphore_signal(barrier, inc=1, device_id=(partner, ket), device_id_type=MESH)
    for m in range(1, n_ket):
        pl.semaphore_signal(barrier, inc=1, device_id=ket_dev(m), device_id_type=MESH)
    pl.semaphore_wait(barrier, n_far + n_ket - 1)

    def order(at):
        if isinstance(at, int):
            return (at + 1) // 2 if at % 2 else (n_far - at // 2) % n_far
        return jnp.where(at % 2 == 1, (at + 1) // 2, (n_far - at // 2) % n_far)

    def far_copy(step):
        return pltpu.make_async_remote_copy(
            src_ref=dens_ref, dst_ref=held.at[bra], send_sem=far_send.at[step - 1],
            recv_sem=far_recv.at[step - 1], device_id=far_dev(step), device_id_type=MESH)

    def column_block(step):
        return lax.rem(far - step + n_far, n_far) * 2

    def pair_copy(step):
        block = column_block(step) + near
        return pltpu.make_async_remote_copy(
            src_ref=held.at[block], dst_ref=held.at[block], send_sem=pair_send.at[step],
            recv_sem=pair_recv.at[step], device_id=(partner, ket), device_id_type=MESH)

    first_copy = pltpu.make_async_remote_copy(
        src_ref=dens_ref, dst_ref=held.at[bra], send_sem=pair_send.at[0],
        recv_sem=pair_recv.at[0], device_id=(partner, ket), device_id_type=MESH)
    first_copy.start()

    for step in [order(at) for at in range(1, n_far)]:
        far_copy(step).start()
    for load in loads:
        load.wait()

    live = live_ref[0, 0]
    rows_b = [tasks_ref[0, 0, 0, t] for t in range(slots)]
    rows_c = [tasks_ref[0, 1, 0, t] for t in range(slots)]
    cols_d = [tasks_ref[0, 2, 0, t] - ket * cols for t in range(slots)]

    def keys_of(rows):
        keys = []
        for t in range(slots):
            rank = jnp.int32(0)
            for before in range(t):
                rank = rank + jnp.where(rows[before] == rows[t], 1, 0)
            keys.append(jnp.where(t < live, rows[t] * named + rank, -1))
        return keys

    keys_b, keys_c = keys_of(rows_b), keys_of(rows_c)
    pairs_b = [rows_b[t] * cols + cols_d[t] + 1 for t in range(slots)]
    pairs_c = [rows_c[t] * cols + cols_d[t] + 1 for t in range(slots)]

    def find(keys, values, want):
        found = jnp.int32(0)
        for t in range(slots):
            found = found + jnp.where(keys[t] == want, values[t], 0)
        return jnp.maximum(found - 1, 0), jnp.where(found > 0, 1.0, 0.0)

    bra_t = jnp.transpose(jnp.concatenate([fit_ref[bra].astype(single), jnp.zeros((lanes - width, points), single)], axis=0)).astype(half)
    ket_f = [fit_ref[ket * cols + d].astype(single) for d in range(cols)]
    coup_t = jnp.transpose(coup_ref[...])

    def holder_of(m):
        return lax.rem(ket + m, n_ket)

    depth = named * padded

    def list_target(s, carry):
        target = holder_of(1 + s // cols) * cols + s % cols
        right = []
        for n in range(named):
            at, scale = find(keys_b, pairs_c, target * named + n)
            pick_b[s, n] = at
            gain_b[s, n] = scale
            at, scale = find(keys_c, pairs_b, target * named + n)
            pick_c[s, n] = at
            right.append(fit_ref[ket * cols + lax.rem(at, cols)].astype(single) * scale)
            right.append(jnp.zeros((padded - width, points), single))
        right.append(jnp.zeros((-depth % lanes, points), single))
        right_all[s] = jnp.transpose(jnp.concatenate(right, axis=0)).astype(half)
        return carry

    def process(block):
        for d in range(cols):
            both = lax.dot_general(held[block, d], fit_ref[block], (((0,), (0,)), ((), ())), preferred_element_type=single)
            fits[block * cols + d] = jnp.sum(both.reshape(width, dens_count, points) * ket_f[d][:, None, :], axis=0)
            for h in range(halves):
                image[d * halves + h] = both[:, h * lanes:(h + 1) * lanes]
            for k in range(dens_count):
                part = jnp.concatenate([image[d * halves + h, pl.ds(k, width, stride=dens_count), :] for h in range(halves)], axis=1)
                part = jnp.concatenate([part, jnp.zeros((padded - width, points), single)], axis=0)
                stack[block * cols + d, k] = part.astype(half)

    lax.fori_loop(0, blocks, list_target, 0)

    def gather_step(at, carry):
        step = order(at)

        @pl.when(at > 0)
        def _():
            far_copy(step).wait_recv()
            pair_copy(step).start()
        process(column_block(step) + near)

        @pl.when(at > 0)
        def _():
            past = order(at - 1)
            pair_copy(past).wait_recv()
            process(column_block(past) + 1 - near)
        return carry

    lax.fori_loop(0, n_far, gather_step, 0)
    pair_copy(order(n_far - 1)).wait_recv()
    process(column_block(order(n_far - 1)) + 1 - near)

    def fit_copy(m):
        return pltpu.make_async_remote_copy(
            src_ref=fit_out.at[m], dst_ref=fit_in.at[m - 1], send_sem=fit_send.at[m - 1],
            recv_sem=fit_recv.at[m - 1], device_id=ket_dev(m), device_id_type=MESH)

    def fit_target(s, carry):
        total = jnp.zeros((dens_count, points), single)
        for n in range(named):
            total += fits[pick_b[s, n]] * gain_b[s, n]
        fit_out[lax.rem(1 + s // cols, n_ket), s % cols] = total
        return carry

    lax.fori_loop(0, blocks, fit_target, 0)
    for m in range(1, n_ket):
        fit_copy(m).start()

    def one_target(s):
        target = holder_of(1 + s // cols) * cols + s % cols
        found = [pick_c[s, n] for n in range(named)]
        right_t = right_all[s][:, :depth]
        for k in range(dens_count):
            left = jnp.concatenate([stack[at, k] for at in found], axis=0)
            heavy = jnp.dot(right_t, left, preferred_element_type=single)
            wide[:, k * points:(k + 1) * points] = (heavy * coup_t).astype(half)
        g_target = fit_ref[target]
        for k in range(dens_count):
            inner[k * width:(k + 1) * width, :] = jnp.dot(
                g_target, wide[:, k * points:(k + 1) * points], preferred_element_type=single)
        last = jnp.dot(inner[...].astype(half), bra_t, preferred_element_type=single)
        for k in range(dens_count):
            spread[pl.ds(k, width, stride=dens_count), :] = last[k * width:(k + 1) * width, :]
        term_out[s] = jnp.transpose(spread[...])[:width].astype(half)

    def term_copy(s):
        return pltpu.make_async_remote_copy(
            src_ref=term_out.at[s], dst_ref=term_in.at[s], send_sem=term_send.at[s],
            recv_sem=term_recv.at[s], device_id=ket_dev(1 + s // cols), device_id_type=MESH)

    away = blocks - cols

    def step_body(s, carry):
        one_target(s)

        @pl.when(s < away)
        def _():
            term_copy(s).start()
        return carry

    lax.fori_loop(0, blocks, step_body, 0)

    for m in range(1, n_ket):
        fit_copy(m).wait_recv()
    for y in range(cols):
        fitted = fit_out[0, y]
        for other in range(n_ket - 1):
            fitted += fit_in[other, y]
        pushed = jnp.dot(fitted, coup_t, precision=lax.Precision.HIGHEST, preferred_element_type=single)
        g_right = fit_ref[ket * cols + y].astype(single)
        rows = (g_right[:, None, :] * pushed[None, :, :]).reshape(flat, points).astype(half)
        out = jnp.dot(rows, bra_t, preferred_element_type=single)
        coul_ref[y] = jnp.transpose(out)[:width].astype(half)
    for s in range(away):
        term_copy(s).wait_recv()
    for y in range(cols):
        exch = term_out[away + y].astype(single)
        for other in range(n_ket - 1):
            exch += term_in[other * cols + y].astype(single)
        exch_ref[y] = exch.astype(half)

    for step in range(1, n_far):
        far_copy(step).wait_send()
    first_copy.wait_send()
    for step in range(1, n_far):
        pair_copy(step).wait_send()
    for m in range(1, n_ket):
        fit_copy(m).wait_send()
    for s in range(away):
        term_copy(s).wait_send()


def per_device(n_bra, n_ket, densities, fit_factors, coupling, quartets, live_count):
    cols, width, flat = densities.shape[1:]
    blocks, points = fit_factors.shape[0], fit_factors.shape[2]
    slots = quartets.shape[2]
    dens_count = flat // width
    named = 2 * slots // blocks
    padded = -(-width // 16) * 16
    dims = (n_bra, n_ket, cols, width, dens_count, points, blocks, slots, named, padded)
    single, half = jnp.float32, jnp.bfloat16
    away = blocks - cols
    vmem = pl.BlockSpec(memory_space=pltpu.VMEM)
    smem = pl.BlockSpec(memory_space=pltpu.SMEM)
    out = jax.ShapeDtypeStruct((cols, width, flat), half)
    dma = pltpu.SemaphoreType.DMA
    coulomb, exchange = pl.pallas_call(
        functools.partial(kernel, dims),
        out_shape=(out, out),
        in_specs=[smem, smem] + [pl.BlockSpec(memory_space=pl.ANY)] * 3,
        out_specs=(vmem, vmem),
        scratch_shapes=[
            pltpu.VMEM((n_bra, cols, width, flat), half),
            pltpu.VMEM((cols * (points // 128), flat, 128), single),
            pltpu.VMEM((blocks * cols, dens_count, padded, points), half),
            pltpu.VMEM((blocks * cols, dens_count, points), single),
            pltpu.VMEM((points, dens_count * points), half),
            pltpu.VMEM((flat, points), single),
            pltpu.VMEM((flat, 128), single),
            pltpu.VMEM((blocks, width, flat), half),
            pltpu.VMEM((away, width, flat), half),
            pltpu.VMEM((n_ket, cols, dens_count, points), single),
            pltpu.VMEM((n_ket - 1, cols, dens_count, points), single),
            pltpu.VMEM((blocks, width, points), half),
            pltpu.VMEM((points, points), single),
            dma((3,)),
            pltpu.VMEM((blocks, points, -(-named * padded // 128) * 128), half),
            pltpu.SMEM((blocks, named), jnp.int32),
            pltpu.SMEM((blocks, named), jnp.int32),
            pltpu.SMEM((blocks, named), single),
            dma((n_bra // 2 - 1,)), dma((n_bra // 2 - 1,)), dma((n_bra // 2,)), dma((n_bra // 2,)),
            dma((away,)), dma((away,)), dma((n_ket - 1,)), dma((n_ket - 1,)),
        ],
        compiler_params=pltpu.CompilerParams(collective_id=0, has_side_effects=True, vmem_limit_bytes=56 * 1024 * 1024),
    )(jnp.transpose(quartets, (0, 3, 1, 2)), live_count, densities[0], fit_factors, coupling)
    return coulomb[None], exchange[None]


def solution(mesh):
    placed = (P("bra", "ket", None, None), P(), P(), P("bra", "ket", None, None), P("bra", "ket"))
    return jax.shard_map(
        functools.partial(per_device, mesh.shape["bra"], mesh.shape["ket"]),
        mesh=mesh,
        in_specs=placed,
        out_specs=(P("bra", "ket", None, None), P("bra", "ket", None, None)),
        check_vma=False,
    )
```
